32 devices in a mesh: outer: 4 (over y, x), inner: 8 (over z, core).
Axes of the slice: x: 2, y: 2, z: 4, core: 2. Of those that a mesh axis runs over, the one named last changes fastest.
Arguments:
- queries: bfloat16 [8192, 1024], P(('outer', 'inner')), may hold values from -6 to 6
- keys: bfloat16 [2, 8192, 1024], P(None, ('outer', 'inner')), may hold values from -6 to 6
- values: bfloat16 [2, 8192, 1024], P(None, ('outer', 'inner')), may hold values from -6 to 6
- betas: float32 [2, 8, 8192], P(None, None, ('outer', 'inner')), may hold values from 0 to 2
- log_decay: float32 [8, 8192], P(None, ('outer', 'inner')), may hold values from -1 to 0
- out_gain: float32 [128], replicated, may hold values from 0.5 to 1.5
Outputs:
- mixed: bfloat16 [8192, 1024], P(('outer', 'inner'))
The draws below stay inside these ranges and needn't reach their ends.
All inputs are finite; a program needn't handle non-finite values.
Results may differ from the reference program's by a relative error of at most 0.0018.
Values sent between devices are 32-bit elements; how exact they have to be, the bound alone decides.
A program may use at most 128 MiB of HBM per device.

```python
import jax
import jax.numpy as jnp
from jax import lax

HEADS = 8
DK = 128
DV = 128
BLOCK_LEN = 64
TOK_DEV = 256
TOKENS = 8192


def head_speed(key):
    order = jax.random.permutation(jax.random.fold_in(key, 101), HEADS)
    quick_count = max(1, HEADS // 2)
    quick = (order < quick_count).astype(jnp.float32)
    device_log = jax.random.uniform(jax.random.fold_in(key, 102), (TOKENS // TOK_DEV,), jnp.float32, jnp.log(0.5), jnp.log(2.0))
    device_factor = jnp.repeat(jnp.exp(device_log), TOK_DEV)
    return (quick, device_factor)


def draw_log_decay(key, part):
    quick, device_factor = head_speed(key)
    quick_rate = jnp.exp(jax.random.uniform(jax.random.fold_in(key, 201), (HEADS, 1), jnp.float32, jnp.log(1.0 / 50.0), jnp.log(1.0 / 30.0)))
    slow_rate = jnp.exp(jax.random.uniform(jax.random.fold_in(key, 202), (HEADS, 1), jnp.float32, jnp.log(0.1), jnp.log(0.4))) / TOKENS
    rate = jnp.where(quick[:, None] > 0.5, quick_rate, slow_rate)
    rough = jax.random.uniform(jax.random.fold_in(key, 203), (HEADS, TOKENS), jnp.float32, 0.5, 1.5)
    base_log = -rate * rough * device_factor[None, :]
    places = jax.random.randint(jax.random.fold_in(key, 204), (2,), 0, TOKENS)
    position = jnp.arange(TOKENS, dtype=jnp.int32)
    struck = jnp.max((position[None, :] == places[:, None]).astype(jnp.float32), 0)
    depth = jax.random.uniform(jax.random.fold_in(key, 205), (HEADS, TOKENS), jnp.float32, jnp.log(0.55), jnp.log(0.8))
    return base_log + struck[None, :] * depth


def draw_betas(key, part):
    quick, device_factor = head_speed(key)
    normal_part = jnp.clip(jax.random.normal(jax.random.fold_in(key, 301), (2, HEADS, TOKENS), jnp.float32), -4.0, 4.0)
    quick_beta = 2.0 * jax.nn.sigmoid(1.2 * normal_part)
    slow_gap = 40.0 / TOKENS * jax.random.uniform(jax.random.fold_in(key, 303), (2, HEADS, TOKENS), jnp.float32, 0.5, 1.5) * device_factor[None, None, :]
    slow_beta = 2.0 - slow_gap
    return jnp.where(quick[None, :, None] > 0.5, quick_beta, slow_beta)


def level_of(own_key, dims, cuts, low, top_value):
    level, own = 1.0, jax.random.fold_in(own_key, 6)
    for dim, parts in cuts:
        draws = jnp.exp(jax.random.uniform(jax.random.fold_in(own, dim), (parts,), jnp.float32, low / len(cuts), top_value / len(cuts)))
        level = level * jnp.repeat(draws, dims[dim] // parts).reshape([-1 if axis == dim else 1 for axis in range(len(dims))])
    return level


def centred(key, dims, scale, limit, cuts=(), held_as=jnp.bfloat16):
    values = scale * jax.random.normal(key, dims, jnp.float32)
    if cuts:
        values = values * level_of(key, dims, cuts, -0.22, 0.18)
    return jnp.clip(values, -limit, limit).astype(held_as)


def setup_inputs(seed: int = 0) -> dict:
    key_list = jax.random.split(jax.random.key(seed), 7)
    return {
        "queries": centred(key_list[0], (TOKENS, HEADS * DK), 1.0, 6.0, ((0, 32),)),
        "keys": centred(key_list[1], (2, TOKENS, HEADS * DK), 1.0, 6.0, ((1, 32),)),
        "values": centred(key_list[2], (2, TOKENS, HEADS * DV), 1.0, 6.0, ((1, 32),)),
        "betas": draw_betas(jax.random.fold_in(key_list[6], 71), 0),
        "log_decay": draw_log_decay(jax.random.fold_in(key_list[6], 71), 0),
        "out_gain": jnp.clip(1.0 + 0.1 * jax.random.normal(key_list[5], (DV,), jnp.float32), 0.5, 1.5),
    }


HIGHEST = lax.Precision.HIGHEST

def prepare(queries, keys, values, betas, log_decay):
    length = queries.shape[0]
    heads = betas.shape[1]
    width_k = queries.shape[1] // heads
    width_v = values.shape[2] // heads
    blocks = length // BLOCK_LEN
    reflect = 2 * BLOCK_LEN
    query_f = queries.astype(jnp.float32).reshape(blocks, BLOCK_LEN, heads, width_k).transpose(0, 2, 1, 3)
    query_inv = lax.rsqrt(lax.optimization_barrier(jnp.sum(query_f * query_f, -1)) + 1e-06)
    query_n = query_f * query_inv[..., None]
    key_f = keys.astype(jnp.float32).reshape(2, blocks, BLOCK_LEN, heads, width_k).transpose(1, 3, 2, 0, 4)
    key_f = key_f.reshape(blocks, heads, reflect, width_k)
    key_inv = lax.rsqrt(lax.optimization_barrier(jnp.sum(key_f * key_f, -1)) + 1e-06)
    key_n = key_f * key_inv[..., None]
    value_n = values.astype(jnp.float32).reshape(2, blocks, BLOCK_LEN, heads, width_v).transpose(1, 3, 2, 0, 4)
    value_n = value_n.reshape(blocks, heads, reflect, width_v)
    beta_r = betas.reshape(2, heads, blocks, BLOCK_LEN).transpose(2, 1, 3, 0).reshape(blocks, heads, reflect)
    decay_t = log_decay.reshape(heads, blocks, BLOCK_LEN).transpose(1, 0, 2)
    decay_r = jnp.stack([decay_t, jnp.zeros_like(decay_t)], -1).reshape(blocks, heads, reflect)
    cumulative = jnp.cumsum(decay_r, -1)
    row_idx = lax.broadcasted_iota(jnp.int32, (reflect, reflect), 0)
    col_idx = lax.broadcasted_iota(jnp.int32, (reflect, reflect), 1)
    key_gram = jnp.einsum('nhrd,nhsd->nhrs', key_f, key_f, precision=HIGHEST) * key_inv[..., :, None] * key_inv[..., None, :]
    fall_off = jnp.exp(jnp.minimum(cumulative[..., :, None] - cumulative[..., None, :], 0.0))
    strict_low = jnp.where(row_idx > col_idx, key_gram * fall_off, 0.0)
    system = jnp.eye(reflect, dtype=jnp.float32) + beta_r[..., :, None] * strict_low
    scaled = jnp.exp(cumulative)
    right_side = jnp.concatenate([(beta_r * scaled)[..., None] * key_n, beta_r[..., None] * value_n], -1)
    solved = lax.linalg.triangular_solve(system, right_side, left_side=True, lower=True, unit_diagonal=True)
    write_key = solved[..., :width_k]
    write_val = solved[..., width_k:]
    tok_idx = lax.broadcasted_iota(jnp.int32, (BLOCK_LEN, reflect), 0)
    ref_idx = lax.broadcasted_iota(jnp.int32, (BLOCK_LEN, reflect), 1)
    query_cum = cumulative.reshape(blocks, heads, BLOCK_LEN, 2)[..., 1]
    query_key = jnp.einsum('nhcd,nhsd->nhcs', query_f, key_f, precision=HIGHEST) * query_inv[..., :, None] * key_inv[..., None, :]
    fade = jnp.exp(jnp.minimum(query_cum[..., :, None] - cumulative[..., None, :], 0.0))
    reach = jnp.where(ref_idx <= 2 * tok_idx + 1, query_key * fade, 0.0)
    reduced = jnp.exp(query_cum)[..., None] * query_n - jnp.einsum('nhcs,nhsd->nhcd', reach, write_key, precision=HIGHEST)
    local_out = jnp.einsum('nhcs,nhsd->nhcd', reach, write_val, precision=HIGHEST)
    last_cum = cumulative[..., -1:]
    tail = jnp.exp(last_cum - cumulative)
    trans = jnp.exp(last_cum)[..., None] * jnp.eye(width_k, dtype=jnp.float32)
    trans = trans - jnp.einsum('nhsd,nhse->nhde', tail[..., None] * write_key, key_n, precision=HIGHEST)
    inject = jnp.einsum('nhsd,nhse->nhde', tail[..., None] * write_val, key_n, precision=HIGHEST)
    return (reduced, local_out, trans, inject)

def finish(readout, out_gain):
    mean_sq = lax.optimization_barrier(jnp.mean(readout * readout, -1, keepdims=True))
    normed = readout * lax.rsqrt(mean_sq + 1e-05) * out_gain
    blocks, heads, span, width_v = normed.shape
    return normed.transpose(0, 2, 1, 3).reshape(blocks * span, heads * width_v).astype(jnp.bfloat16)

def reference(queries, keys, values, betas, log_decay, out_gain):
    groups = TOKENS // TOK_DEV
    query_g = queries.reshape(groups, TOK_DEV, HEADS * DK)
    key_g = keys.reshape(2, groups, TOK_DEV, HEADS * DK).transpose(1, 0, 2, 3)
    value_g = values.reshape(2, groups, TOK_DEV, HEADS * DV).transpose(1, 0, 2, 3)
    beta_g = betas.reshape(2, HEADS, groups, TOK_DEV).transpose(2, 0, 1, 3)
    decay_g = log_decay.reshape(HEADS, groups, TOK_DEV).transpose(1, 0, 2)

    def group_step(state, inputs):
        reduced, local_out, trans, inject = prepare(*inputs)

        def block_step(inner_state, pieces):
            red_b, loc_b, trans_b, inj_b = pieces
            readout = jnp.einsum('hcd,hed->hce', red_b, inner_state, precision=HIGHEST) + loc_b
            next_state = jnp.einsum('hde,hef->hdf', inner_state, trans_b, precision=HIGHEST) + inj_b
            return (next_state, readout)
        state, readouts = lax.scan(block_step, state, (reduced, local_out, trans, inject))
        return (state, finish(readouts, out_gain))
    start = jnp.zeros((HEADS, DV, DK), jnp.float32)
    final_state, outputs = lax.scan(group_step, start, (query_g, key_g, value_g, beta_g, decay_g))
    return outputs.reshape(TOKENS, HEADS * DV)
```

```python
import functools

import jax
import jax.numpy as jnp
from jax import lax
from jax.experimental import pallas as pl
from jax.experimental.pallas import tpu as pltpu
from jax.sharding import PartitionSpec as P

BLOCK_LEN = 64
F32 = jnp.float32
BF16 = jnp.bfloat16


def split(x):
    high = x.astype(BF16)
    low = (x - high.astype(F32)).astype(BF16)
    return high, low


def dot(a, b):
    return lax.dot_general(a, b, (((1,), (0,)), ((), ())), preferred_element_type=F32)


def dot_t(a, b):
    return lax.dot_general(a, b, (((1,), (1,)), ((), ())), preferred_element_type=F32)


def wide(x):
    return jnp.concatenate(split(x), 1)


def mul(a, b):
    a2 = wide(a)
    bh, bl = split(b)
    if b.shape[1] == 128:
        row = jnp.concatenate([bh, bl], 1)
        both = dot(a2, jnp.concatenate([row, row], 0))
        return both[:, :128] + both[:, 128:]
    return dot(a2, jnp.concatenate([bh, bh], 0)) + dot(a2[:, :128], bl)


def mul_left(a, b):
    return dot(wide(a), jnp.concatenate([b, b], 0))


def add_right(x, y):
    return jnp.concatenate([x[:, :128], x[:, 128:] + y], 1)


def local_kernel(blocks, q_ref, k_ref, v_ref, s_ref, x_ref, c_ref, b_ref):
    span = BLOCK_LEN
    size = 2 * span
    row = lax.broadcasted_iota(jnp.int32, (size, size), 0)
    col = lax.broadcasted_iota(jnp.int32, (size, size), 1)
    row_t, col_t = row % span, col % span
    row_rank, col_rank = 2 * row_t + row // span, 2 * col_t + col // span
    eye = row == col
    eye_f = eye.astype(F32)
    lower = row_rank > col_rank
    c_mask = (col_t <= row_t) & (col < span)
    r_mask = (row_t <= col_t) & (row < span)
    levels = []
    width = 1
    while width < size:
        levels.append(
            (row_rank // (2 * width) == col_rank // (2 * width))
            & (row_rank // width != col_rank // width)
            & lower
        )
        width *= 2

    work = []
    for n in range(blocks):
        at = pl.ds(n * span, span)
        q_b = q_ref[at, :]
        k_b = jnp.concatenate([k_ref[0, at, :], k_ref[1, at, :]], 0)
        v_b = jnp.concatenate([v_ref[0, at, :], v_ref[1, at, :]], 0)
        d_row = s_ref[0, n : n + 1, :]
        beta_row = s_ref[0, blocks + n : blocks + n + 1, :]
        d_col = jnp.sum(jnp.where(eye, d_row, 0.0), 1, keepdims=True)
        beta_col = jnp.sum(jnp.where(eye, beta_row, 0.0), 1, keepdims=True)
        c_col = jnp.sum(jnp.where(c_mask, d_row, 0.0), 1, keepdims=True)
        c_row = jnp.sum(jnp.where(r_mask, d_col, 0.0), 0, keepdims=True)
        gram = dot_t(k_b, k_b)
        k_f = k_b.astype(F32)
        q_f = q_b.astype(F32)
        ki_col = lax.rsqrt(jnp.sum(k_f * k_f, 1, keepdims=True) + 1e-06)
        ki_row = lax.rsqrt(jnp.sum(jnp.where(eye, gram, 0.0), 0, keepdims=True) + 1e-06)
        qi_col = lax.rsqrt(jnp.sum(q_f * q_f, 1, keepdims=True) + 1e-06)
        fall = jnp.exp(jnp.minimum(c_col - c_row, 0.0))
        low = jnp.where(lower, gram * (beta_col * ki_col) * ki_row * fall, 0.0)
        reach = dot_t(q_b, k_b) * qi_col * ki_row * fall[:span]
        reach = jnp.where(col_t[:span] <= row_t[:span], reach, 0.0)
        query = q_f * (qi_col * jnp.exp(c_col[:span]))
        work.append((k_b, v_b, beta_row, c_row, c_col, ki_row, ki_col, low, reach, query))

    inverse = [eye_f - jnp.where(levels[0], w[7], 0.0) for w in work]
    for mask in levels[1:]:
        part = [mul(jnp.where(mask, w[7], 0.0), t) for w, t in zip(work, inverse)]
        inverse = [t - mul(t, p) for t, p in zip(inverse, part)]

    state = None
    for n in range(blocks):
        k_b, v_b, beta_row, c_row, c_col, ki_row, ki_col, low, reach, query = work[n]
        t = inverse[n] * beta_row
        written = jnp.concatenate(
            [mul_left(t * (ki_row * jnp.exp(c_row)), k_b), mul_left(t, v_b)], 1
        )
        got = mul(reach, written)
        reduced, local_out = query - got[:, :128], got[:, 128:]
        last = c_col[span - 1 : span, :]
        tail = jnp.exp(last - c_col) * ki_col
        wh, wl = split(written * tail)
        k_t = jnp.transpose(k_b.astype(F32)).astype(BF16)
        made = dot(jnp.concatenate([k_t, k_t], 1), jnp.concatenate([wh, wl], 0))
        trans = jnp.exp(last) * eye_f - made[:, :128]
        inject = made[:, 128:]
        at = pl.ds(n * span, span)
        if state is None:
            c_ref[0, at, :] = reduced
            b_ref[0, at, :] = local_out
            state = jnp.concatenate([trans, inject], 1)
        else:
            read = mul(reduced, state)
            c_ref[0, at, :] = read[:, :128]
            b_ref[0, at, :] = read[:, 128:] + local_out
            state = add_right(mul(trans, state), inject)
    x_ref[0] = state


def local_phase(queries, keys, values, betas, log_decay):
    length = queries.shape[0]
    heads = betas.shape[1]
    blocks = length // BLOCK_LEN
    beta = betas.reshape(2, heads, blocks, BLOCK_LEN).transpose(1, 2, 0, 3)
    beta = beta.reshape(heads, blocks, 2 * BLOCK_LEN)
    decay = log_decay.reshape(heads, blocks, 1, BLOCK_LEN)
    decay = jnp.concatenate([decay, decay], 2).reshape(heads, blocks, 2 * BLOCK_LEN)
    small = jnp.concatenate([decay, beta], 1)
    return pl.pallas_call(
        functools.partial(local_kernel, blocks),
        grid=(heads,),
        in_specs=[
            pl.BlockSpec((length, 128), lambda h: (0, h)),
            pl.BlockSpec((2, length, 128), lambda h: (0, 0, h)),
            pl.BlockSpec((2, length, 128), lambda h: (0, 0, h)),
            pl.BlockSpec((1, 2 * blocks, 128), lambda h: (h, 0, 0)),
        ],
        out_specs=[
            pl.BlockSpec((1, 128, 256), lambda h: (h, 0, 0)),
            pl.BlockSpec((1, length, 128), lambda h: (h, 0, 0)),
            pl.BlockSpec((1, length, 128), lambda h: (h, 0, 0)),
        ],
        out_shape=[
            jax.ShapeDtypeStruct((heads, 128, 256), F32),
            jax.ShapeDtypeStruct((heads, length, 128), F32),
            jax.ShapeDtypeStruct((heads, length, 128), F32),
        ],
        name="local_phase",
    )(queries, keys, values, small)


def then(earlier, later):
    return add_right(mul(later[:, :128], earlier), later[:, 128:])


def exchange_kernel(
    inner, outer, x_ref, e_ref, got, groups, mine, ready, came,
    send1, recv1, send2, recv2, send3, recv3,
):
    me = lax.axis_index("inner")
    group = lax.axis_index("outer")
    barrier = pltpu.get_barrier_semaphore()
    for d in range(1, inner):
        pl.semaphore_signal(
            barrier, inc=1, device_id=(group, (me + d) % inner),
            device_id_type=pl.DeviceIdType.MESH,
        )
    for d in range(1, outer):
        pl.semaphore_signal(
            barrier, inc=1, device_id=((group + d) % outer, me),
            device_id_type=pl.DeviceIdType.MESH,
        )
    pl.semaphore_wait(barrier, inner + outer - 2)

    first = []
    for d in range(1, inner):
        to = (me + d) % inner
        copy = pltpu.make_async_remote_copy(
            src_ref=x_ref.at[to], dst_ref=got.at[d],
            send_sem=send1.at[d], recv_sem=recv1.at[d],
            device_id=(group, to), device_id_type=pl.DeviceIdType.MESH,
        )
        copy.start()
        first.append(copy)
    got[0] = x_ref[me]
    for copy in first:
        copy.wait()

    before = [None]
    state = got[me]
    for i in range(1, inner + 1):
        before.append(state)
        if i < inner:
            state = then(state, got[(me - i + inner) % inner])
    total = before[inner]
    mine[...] = total

    second = []
    for d in range(1, outer):
        copy = pltpu.make_async_remote_copy(
            src_ref=mine, dst_ref=groups.at[d],
            send_sem=send2.at[d], recv_sem=recv2.at[d],
            device_id=((group + d) % outer, me), device_id_type=pl.DeviceIdType.MESH,
        )
        copy.start()
        second.append(copy)
    groups[0] = total
    for copy in second:
        copy.wait()
    start = jnp.zeros((128, 128), F32)
    for g in range(outer - 1):
        pair = groups[(group - g + outer) % outer]
        moved = mul(pair[:, :128], start) + pair[:, 128:]
        start = jnp.where(g < group, moved, start)

    ready[0] = start
    for i in range(1, inner):
        ready[i] = mul(before[i][:, :128], start) + before[i][:, 128:]
    third = []
    for d in range(1, inner):
        to = (me + d) % inner
        copy = pltpu.make_async_remote_copy(
            src_ref=ready.at[to], dst_ref=came.at[me],
            send_sem=send3.at[d], recv_sem=recv3.at[d],
            device_id=(group, to), device_id_type=pl.DeviceIdType.MESH,
        )
        copy.start()
        third.append(copy)
    e_ref[me] = ready[me]
    for copy in third:
        copy.wait()
    for d in range(1, inner):
        frm = (me + d) % inner
        e_ref[frm] = came[frm]


def exchange(pairs, inner, outer):
    heads = pairs.shape[0]
    vmem = pl.BlockSpec(memory_space=pltpu.VMEM)
    dma = pltpu.SemaphoreType.DMA
    return pl.pallas_call(
        functools.partial(exchange_kernel, inner, outer),
        in_specs=[vmem],
        out_specs=vmem,
        out_shape=jax.ShapeDtypeStruct((heads, 128, 128), F32),
        scratch_shapes=[
            pltpu.VMEM((inner, 128, 256), F32),
            pltpu.VMEM((outer, 128, 256), F32),
            pltpu.VMEM((128, 256), F32),
            pltpu.VMEM((inner, 128, 128), F32),
            pltpu.VMEM((inner, 128, 128), F32),
            dma((inner,)), dma((inner,)),
            dma((outer,)), dma((outer,)),
            dma((inner,)), dma((inner,)),
        ],
        compiler_params=pltpu.CompilerParams(collective_id=0, has_side_effects=True),
        name="exchange",
    )(pairs)


HIGHEST = lax.Precision.HIGHEST


def join(earlier, later):
    moved = jnp.einsum("hde,hef->hdf", later[..., :128], earlier, precision=HIGHEST)
    return jnp.concatenate([moved[..., :128], moved[..., 128:] + later[..., 128:]], -1)


def entering(pairs, axis, begin):
    gathered = lax.all_gather(pairs, axis)

    def one(hop, state):
        return join(state, lax.dynamic_index_in_dim(gathered, hop, 0, False))

    return lax.fori_loop(0, lax.axis_index(axis), one, begin)


def exchange_plain(pairs):
    eye = jnp.concatenate([jnp.eye(128, dtype=F32), jnp.zeros((128, 128), F32)], 1)
    begin = jnp.zeros_like(pairs) + eye
    before = entering(pairs, "inner", begin)
    through = join(before, pairs)
    last = lax.axis_index("inner") == lax.axis_size("inner") - 1
    total = lax.psum(jnp.where(last, through, 0.0), "inner")
    start = entering(total, "outer", begin)
    return join(start, before)[..., 128:]


def finish_kernel(c_ref, b_ref, e_ref, g_ref, o_ref):
    readout = mul(c_ref[0], e_ref[0]) + b_ref[0]
    mean_sq = jnp.mean(readout * readout, 1, keepdims=True)
    o_ref[...] = (readout * lax.rsqrt(mean_sq + 1e-05) * g_ref[...]).astype(BF16)


def finish(carried, base, state, out_gain):
    heads, length, _ = carried.shape
    return pl.pallas_call(
        finish_kernel,
        grid=(heads,),
        in_specs=[
            pl.BlockSpec((1, length, 128), lambda h: (h, 0, 0)),
            pl.BlockSpec((1, length, 128), lambda h: (h, 0, 0)),
            pl.BlockSpec((1, 128, 128), lambda h: (h, 0, 0)),
            pl.BlockSpec((1, 128), lambda h: (0, 0)),
        ],
        out_specs=pl.BlockSpec((length, 128), lambda h: (0, h)),
        out_shape=jax.ShapeDtypeStruct((length, heads * 128), BF16),
        name="finish",
    )(carried, base, state, out_gain.reshape(1, 128))


def per_device(inner, outer, queries, keys, values, betas, log_decay, out_gain):
    heads = betas.shape[1]
    pairs, carried, base = local_phase(queries, keys, values, betas, log_decay)
    if inner == heads:
        state = exchange(pairs, inner, outer)
    else:
        state = exchange_plain(pairs)
    return finish(carried, base, state, out_gain)


def solution(mesh):
    both = ("outer", "inner")
    placed = (P(both, None), P(None, both, None), P(None, both, None), P(None, None, both), P(None, both), P())
    return jax.shard_map(
        functools.partial(per_device, mesh.shape["inner"], mesh.shape["outer"]),
        mesh=mesh,
        in_specs=placed,
        out_specs=P(both, None),
        check_vma=False,
    )
```

```python
import functools

import jax
import jax.numpy as jnp
from jax import lax
from jax.experimental import pallas as pl
from jax.experimental.pallas import tpu as pltpu
from jax.sharding import PartitionSpec as P

BLOCK_LEN = 64
F32 = jnp.float32
BF16 = jnp.bfloat16


def split(x):
    high = x.astype(BF16)
    low = (x - high.astype(F32)).astype(BF16)
    return high, low


def dot(a, b):
    return lax.dot_general(a, b, (((1,), (0,)), ((), ())), preferred_element_type=F32)


def dot_t(a, b):
    return lax.dot_general(a, b, (((1,), (1,)), ((), ())), preferred_element_type=F32)


def wide(x):
    return jnp.concatenate(split(x), 1)


def mul(a, b):
    a2 = wide(a)
    bh, bl = split(b)
    if b.shape[1] == 128:
        row = jnp.concatenate([bh, bl], 1)
        both = dot(a2, jnp.concatenate([row, row], 0))
        return both[:, :128] + both[:, 128:]
    return dot(a2, jnp.concatenate([bh, bh], 0)) + dot(a2[:, :128], bl)


def mul_left(a, b):
    return dot(wide(a), jnp.concatenate([b, b], 0))


def add_right(x, y):
    return jnp.concatenate([x[:, :128], x[:, 128:] + y], 1)


def masks():
    span = BLOCK_LEN
    size = 2 * span
    row = lax.broadcasted_iota(jnp.int32, (size, size), 0)
    col = lax.broadcasted_iota(jnp.int32, (size, size), 1)
    row_t, col_t = row % span, col % span
    row_rank, col_rank = 2 * row_t + row // span, 2 * col_t + col // span
    eye = row == col
    eye_f = eye.astype(F32)
    lower = row_rank > col_rank
    c_mask = (col_t <= row_t) & (col < span)
    r_mask = (row_t <= col_t) & (row < span)
    levels = []
    width = 1
    while width < size:
        levels.append(
            (row_rank // (2 * width) == col_rank // (2 * width))
            & (row_rank // width != col_rank // width)
            & lower
        )
        width *= 2

    return row, col_t, row_t, eye, eye_f, lower, c_mask, r_mask, levels


def head_maps(blocks, heads_in, load, emit):
    span = BLOCK_LEN
    row, col_t, row_t, eye, eye_f, lower, c_mask, r_mask, levels = masks()
    work = []
    for i, n in [(i, n) for i in range(heads_in) for n in range(blocks)]:
        q_b, k_b, v_b, d_row, beta_row = load(i, n)
        d_col = jnp.sum(jnp.where(eye, d_row, 0.0), 1, keepdims=True)
        beta_col = jnp.sum(jnp.where(eye, beta_row, 0.0), 1, keepdims=True)
        c_col = jnp.sum(jnp.where(c_mask, d_row, 0.0), 1, keepdims=True)
        c_row = jnp.sum(jnp.where(r_mask, d_col, 0.0), 0, keepdims=True)
        gram = dot_t(k_b, k_b)
        k_f = k_b.astype(F32)
        q_f = q_b.astype(F32)
        ki_col = lax.rsqrt(jnp.sum(k_f * k_f, 1, keepdims=True) + 1e-06)
        ki_row = lax.rsqrt(jnp.sum(jnp.where(eye, gram, 0.0), 0, keepdims=True) + 1e-06)
        qi_col = lax.rsqrt(jnp.sum(q_f * q_f, 1, keepdims=True) + 1e-06)
        fall = jnp.exp(jnp.minimum(c_col - c_row, 0.0))
        low = jnp.where(lower, gram * (beta_col * ki_col) * ki_row * fall, 0.0)
        reach = dot_t(q_b, k_b) * qi_col * ki_row * fall[:span]
        reach = jnp.where(col_t[:span] <= row_t[:span], reach, 0.0)
        query = q_f * (qi_col * jnp.exp(c_col[:span]))
        work.append((k_b, v_b, beta_row, c_row, c_col, ki_row, ki_col, low, reach, query))

    inverse = [eye_f - jnp.where(levels[0], w[7], 0.0) for w in work]
    for mask in levels[1:]:
        part = [mul(jnp.where(mask, w[7], 0.0), t) for w, t in zip(work, inverse)]
        inverse = [t - mul(t, p) for t, p in zip(inverse, part)]

    states = [None] * heads_in
    for n in range(blocks):
        for i in range(heads_in):
            state = states[i]
            k_b, v_b, beta_row, c_row, c_col, ki_row, ki_col, low, reach, query = work[i * blocks + n]
            t = inverse[i * blocks + n] * beta_row
            written = jnp.concatenate(
                [mul_left(t * (ki_row * jnp.exp(c_row)), k_b), mul_left(t, v_b)], 1
            )
            got = mul(reach, written)
            reduced, local_out = query - got[:, :128], got[:, 128:]
            last = c_col[span - 1 : span, :]
            tail = jnp.exp(last - c_col) * ki_col
            wh, wl = split(written * tail)
            k_t = jnp.transpose(k_b.astype(F32)).astype(BF16)
            made = dot(jnp.concatenate([k_t, k_t], 1), jnp.concatenate([wh, wl], 0))
            trans = jnp.exp(last) * eye_f - made[:, :128]
            inject = made[:, 128:]
            if state is None:
                emit(i, n, reduced, local_out)
                states[i] = jnp.concatenate([trans, inject], 1)
            else:
                read = mul(reduced, state)
                emit(i, n, read[:, :128], read[:, 128:] + local_out)
                states[i] = add_right(mul(trans, state), inject)
    return states


def local_kernel(blocks, q_ref, k_ref, v_ref, s_ref, x_ref, c_ref, b_ref):
    def load(i, n):
        at = pl.ds(n * BLOCK_LEN, BLOCK_LEN)
        k_b = jnp.concatenate([k_ref[0, at, :], k_ref[1, at, :]], 0)
        v_b = jnp.concatenate([v_ref[0, at, :], v_ref[1, at, :]], 0)
        return q_ref[at, :], k_b, v_b, s_ref[0, n : n + 1, :], s_ref[0, blocks + n : blocks + n + 1, :]

    def emit(i, n, carried, base):
        at = pl.ds(n * BLOCK_LEN, BLOCK_LEN)
        c_ref[0, at, :] = carried
        b_ref[0, at, :] = base

    x_ref[0] = head_maps(blocks, 1, load, emit)[0]


def small_rows(betas, log_decay):
    heads, length = log_decay.shape
    blocks = length // BLOCK_LEN
    beta = betas.reshape(2, heads, blocks, BLOCK_LEN).transpose(1, 2, 0, 3)
    beta = beta.reshape(heads, blocks, 2 * BLOCK_LEN)
    decay = log_decay.reshape(heads, blocks, 1, BLOCK_LEN)
    decay = jnp.concatenate([decay, decay], 2).reshape(heads, blocks, 2 * BLOCK_LEN)
    small = jnp.concatenate([decay, beta], 1)
    return small


def local_phase(queries, keys, values, betas, log_decay):
    length = queries.shape[0]
    heads = betas.shape[1]
    blocks = length // BLOCK_LEN
    small = small_rows(betas, log_decay)
    return pl.pallas_call(
        functools.partial(local_kernel, blocks),
        grid=(heads,),
        in_specs=[
            pl.BlockSpec((length, 128), lambda h: (0, h)),
            pl.BlockSpec((2, length, 128), lambda h: (0, 0, h)),
            pl.BlockSpec((2, length, 128), lambda h: (0, 0, h)),
            pl.BlockSpec((1, 2 * blocks, 128), lambda h: (h, 0, 0)),
        ],
        out_specs=[
            pl.BlockSpec((1, 128, 256), lambda h: (h, 0, 0)),
            pl.BlockSpec((1, length, 128), lambda h: (h, 0, 0)),
            pl.BlockSpec((1, length, 128), lambda h: (h, 0, 0)),
        ],
        out_shape=[
            jax.ShapeDtypeStruct((heads, 128, 256), F32),
            jax.ShapeDtypeStruct((heads, length, 128), F32),
            jax.ShapeDtypeStruct((heads, length, 128), F32),
        ],
        name="local_phase",
    )(queries, keys, values, small)


def then(earlier, later):
    return add_right(mul(later[:, :128], earlier), later[:, 128:])


TOGETHER = 2


def normed(carried, base, state, gain):
    readout = mul(carried, state) + base
    mean_sq = jnp.mean(readout * readout, 1, keepdims=True)
    return (readout * lax.rsqrt(mean_sq + 1e-05) * gain).astype(BF16)


def whole_kernel(
    inner, outer, q_ref, k_ref, v_ref, s_ref, g_ref, o_ref,
    sent, got, groups, mine, ready, came, c_buf, b_buf,
    send1, recv1, send2, recv2, send3, recv3,
):
    mesh_id = pl.DeviceIdType.MESH
    length = q_ref.shape[0]
    blocks = length // BLOCK_LEN
    me = lax.axis_index("inner")
    group = lax.axis_index("outer")
    groups[...] = jnp.zeros_like(groups)
    barrier = pltpu.get_barrier_semaphore()
    for d in range(1, inner):
        pl.semaphore_signal(barrier, inc=1, device_id=(group, (me + d) % inner), device_id_type=mesh_id)
    for d in range(1, outer):
        pl.semaphore_signal(barrier, inc=1, device_id=((group + d) % outer, me), device_id_type=mesh_id)
    pl.semaphore_wait(barrier, inner + outer - 2)

    def map_copy(slot):
        to = (me + slot) % inner
        return pltpu.make_async_remote_copy(
            src_ref=sent.at[slot], dst_ref=got.at[slot],
            send_sem=send1.at[slot], recv_sem=recv1.at[slot],
            device_id=(group, to), device_id_type=mesh_id,
        )

    def step(turn, carry):
        places = [turn * TOGETHER + i + 1 for i in range(TOGETHER)]
        heads = [(me + p) % inner for p in places]

        def load(i, n):
            at = pl.ds(n * BLOCK_LEN, BLOCK_LEN)
            lanes = pl.ds(pl.multiple_of(heads[i] * 128, 128), 128)
            k_b = jnp.concatenate([k_ref[0, at, lanes], k_ref[1, at, lanes]], 0)
            v_b = jnp.concatenate([v_ref[0, at, lanes], v_ref[1, at, lanes]], 0)
            rows = s_ref[heads[i]]
            return q_ref[at, lanes], k_b, v_b, rows[n : n + 1], rows[blocks + n : blocks + n + 1]

        def emit(i, n, carried, base):
            at = pl.ds(n * BLOCK_LEN, BLOCK_LEN)
            c_buf[heads[i], at, :] = carried
            b_buf[heads[i], at, :] = base

        states = head_maps(blocks, TOGETHER, load, emit)
        for i in range(TOGETHER):
            sent[places[i]] = states[i]
            if i < TOGETHER - 1:
                map_copy(places[i]).start()
            else:

                @pl.when(places[i] < inner)
                def _():
                    map_copy(places[i]).start()

        return carry

    lax.fori_loop(0, inner // TOGETHER, step, 0)
    got[0] = sent[inner]
    for slot in range(1, inner):
        map_copy(slot).wait()

    maps = [got[(me - i + inner) % inner] for i in range(inner)]

    def tree(parts):
        if len(parts) == 1:
            return parts
        half = len(parts) // 2
        pairs = [then(parts[2 * i], parts[2 * i + 1]) for i in range(half)]
        return pairs

    level = maps
    levels = [maps]
    while len(level) > 1:
        level = tree(level)
        levels.append(level)
    mine[...] = level[0]

    def group_copy(d):
        return pltpu.make_async_remote_copy(
            src_ref=mine, dst_ref=groups.at[d],
            send_sem=send2.at[d], recv_sem=recv2.at[d],
            device_id=((group + d) % outer, me), device_id_type=mesh_id,
        )

    for d in range(1, outer):

        @pl.when(group + d < outer)
        def _():
            group_copy(d).start()

    before = {}
    for i in range(1, inner):
        low = i & -i
        height = low.bit_length() - 1
        part = levels[height][(i - low) >> height]
        before[i] = part if i == low else then(before[i - low], part)
    left = wide(jnp.concatenate([before[i][:, :128] for i in range(1, inner)], 0))
    right = jnp.concatenate([before[i][:, 128:] for i in range(1, inner)], 0)

    for d in range(1, outer):

        @pl.when(group + d < outer)
        def _():
            group_copy(d).wait_send()

        @pl.when(group - d >= 0)
        def _():
            group_copy(d).wait_recv()

    start = jnp.zeros((128, 128), F32)
    for g in range(outer - 1):
        pair = groups[(group - g + outer) % outer]
        moved = mul(pair[:, :128], start) + pair[:, 128:]
        start = jnp.where(g < group, moved, start)

    sh, sl = split(start)
    row = jnp.concatenate([sh, sl], 1)
    both = dot(left, jnp.concatenate([row, row], 0))
    ready[0] = start
    ready[pl.ds(1, inner - 1)] = (both[:, :128] + both[:, 128:] + right).reshape(inner - 1, 128, 128)

    def back_copy(d):
        to = (me + d) % inner
        return pltpu.make_async_remote_copy(
            src_ref=ready.at[to], dst_ref=came.at[d],
            send_sem=send3.at[d], recv_sem=recv3.at[d],
            device_id=(group, to), device_id_type=mesh_id,
        )

    for d in range(1, inner):
        back_copy(d).start()
    came[0] = ready[me]

    def out(d):
        head = (me - d + inner) % inner
        lanes = pl.ds(pl.multiple_of(head * 128, 128), 128)
        o_ref[:, lanes] = normed(c_buf[head], b_buf[head], came[d], g_ref[...])

    out(0)
    for first in range(1, inner, 2):
        some = range(first, min(first + 2, inner))
        for d in some:
            back_copy(d).wait()
        for d in some:
            out(d)


def whole(inner, outer, queries, keys, values, betas, log_decay, out_gain):
    length, width = queries.shape
    vmem = pl.BlockSpec(memory_space=pltpu.VMEM)
    dma = pltpu.SemaphoreType.DMA
    return pl.pallas_call(
        functools.partial(whole_kernel, inner, outer),
        in_specs=[vmem] * 5,
        out_specs=vmem,
        out_shape=jax.ShapeDtypeStruct((length, width), BF16),
        scratch_shapes=[
            pltpu.VMEM((inner + 1, 128, 256), F32),
            pltpu.VMEM((inner, 128, 256), F32),
            pltpu.VMEM((outer, 128, 256), F32),
            pltpu.VMEM((128, 256), F32),
            pltpu.VMEM((inner, 128, 128), F32),
            pltpu.VMEM((inner, 128, 128), F32),
            pltpu.VMEM((inner, length, 128), F32),
            pltpu.VMEM((inner, length, 128), F32),
            dma((inner,)), dma((inner,)),
            dma((outer,)), dma((outer,)),
            dma((inner,)), dma((inner,)),
        ],
        compiler_params=pltpu.CompilerParams(collective_id=0, has_side_effects=True),
        name="whole",
    )(queries, keys, values, small_rows(betas, log_decay), out_gain.reshape(1, 128))


HIGHEST = lax.Precision.HIGHEST


def join(earlier, later):
    moved = jnp.einsum("hde,hef->hdf", later[..., :128], earlier, precision=HIGHEST)
    return jnp.concatenate([moved[..., :128], moved[..., 128:] + later[..., 128:]], -1)


def entering(pairs, axis, begin):
    gathered = lax.all_gather(pairs, axis)

    def one(hop, state):
        return join(state, lax.dynamic_index_in_dim(gathered, hop, 0, False))

    return lax.fori_loop(0, lax.axis_index(axis), one, begin)


def exchange_plain(pairs):
    eye = jnp.concatenate([jnp.eye(128, dtype=F32), jnp.zeros((128, 128), F32)], 1)
    begin = jnp.zeros_like(pairs) + eye
    before = entering(pairs, "inner", begin)
    through = join(before, pairs)
    last = lax.axis_index("inner") == lax.axis_size("inner") - 1
    total = lax.psum(jnp.where(last, through, 0.0), "inner")
    start = entering(total, "outer", begin)
    return join(start, before)[..., 128:]


def finish_kernel(c_ref, b_ref, e_ref, g_ref, o_ref):
    readout = mul(c_ref[0], e_ref[0]) + b_ref[0]
    mean_sq = jnp.mean(readout * readout, 1, keepdims=True)
    o_ref[...] = (readout * lax.rsqrt(mean_sq + 1e-05) * g_ref[...]).astype(BF16)


def finish(carried, base, state, out_gain):
    heads, length, _ = carried.shape
    return pl.pallas_call(
        finish_kernel,
        grid=(heads,),
        in_specs=[
            pl.BlockSpec((1, length, 128), lambda h: (h, 0, 0)),
            pl.BlockSpec((1, length, 128), lambda h: (h, 0, 0)),
            pl.BlockSpec((1, 128, 128), lambda h: (h, 0, 0)),
            pl.BlockSpec((1, 128), lambda h: (0, 0)),
        ],
        out_specs=pl.BlockSpec((length, 128), lambda h: (0, h)),
        out_shape=jax.ShapeDtypeStruct((length, heads * 128), BF16),
        name="finish",
    )(carried, base, state, out_gain.reshape(1, 128))


def per_device(inner, outer, queries, keys, values, betas, log_decay, out_gain):
    heads = betas.shape[1]
    if inner == heads:
        return whole(inner, outer, queries, keys, values, betas, log_decay, out_gain)
    pairs, carried, base = local_phase(queries, keys, values, betas, log_decay)
    return finish(carried, base, exchange_plain(pairs), out_gain)


def solution(mesh):
    both = ("outer", "inner")
    placed = (P(both, None), P(None, both, None), P(None, both, None), P(None, None, both), P(None, both), P())
    return jax.shard_map(
        functools.partial(per_device, mesh.shape["inner"], mesh.shape["outer"]),
        mesh=mesh,
        in_specs=placed,
        out_specs=P(both, None),
        check_vma=False,
    )
```

```python
import functools

import jax
import jax.numpy as jnp
from jax import lax
from jax.experimental import pallas as pl
from jax.experimental.pallas import tpu as pltpu
from jax.sharding import PartitionSpec as P

BLOCK_LEN = 64
F32 = jnp.float32
BF16 = jnp.bfloat16


def split(x):
    high = x.astype(BF16)
    low = (x - high.astype(F32)).astype(BF16)
    return high, low


def dot(a, b):
    return lax.dot_general(a, b, (((1,), (0,)), ((), ())), preferred_element_type=F32)


def dot_t(a, b):
    return lax.dot_general(a, b, (((1,), (1,)), ((), ())), preferred_element_type=F32)


def wide(x):
    return jnp.concatenate(split(x), 1)


def mul(a, b):
    a2 = wide(a)
    bh, bl = split(b)
    if b.shape[1] == 128:
        row = jnp.concatenate([bh, bl], 1)
        both = dot(a2, jnp.concatenate([row, row], 0))
        return both[:, :128] + both[:, 128:]
    return dot(a2, jnp.concatenate([bh, bh], 0)) + dot(a2[:, :128], bl)


def mul_left(a, b):
    return dot(wide(a), jnp.concatenate([b, b], 0))


def add_right(x, y):
    return jnp.concatenate([x[:, :128], x[:, 128:] + y], 1)


def masks():
    span = BLOCK_LEN
    size = 2 * span
    row = lax.broadcasted_iota(jnp.int32, (size, size), 0)
    col = lax.broadcasted_iota(jnp.int32, (size, size), 1)
    row_t, col_t = row & (span - 1), col & (span - 1)
    row_rank = 2 * row_t + (row >= span).astype(jnp.int32)
    col_rank = 2 * col_t + (col >= span).astype(jnp.int32)
    differ = row_rank ^ col_rank
    eye = row == col
    eye_f = eye.astype(F32)
    lower = row_rank > col_rank
    c_mask = (col_t <= row_t) & (col < span)
    r_mask = (row_t <= col_t) & (row < span)
    levels = []
    width = 1
    while width < size:
        levels.append(
            (differ >= width) & (differ < 2 * width) & lower
        )
        width *= 2

    return row, col_t, row_t, eye, eye_f, lower, c_mask, r_mask, levels


def head_maps(blocks, heads_in, load, emit):
    span = BLOCK_LEN
    row, col_t, row_t, eye, eye_f, lower, c_mask, r_mask, levels = masks()
    work = []
    for i, n in [(i, n) for i in range(heads_in) for n in range(blocks)]:
        q_b, k_b, v_b, d_row, beta_row = load(i, n)
        d_col = jnp.sum(jnp.where(eye, d_row, 0.0), 1, keepdims=True)
        beta_col = jnp.sum(jnp.where(eye, beta_row, 0.0), 1, keepdims=True)
        c_col = jnp.sum(jnp.where(c_mask, d_row, 0.0), 1, keepdims=True)
        c_row = jnp.sum(jnp.where(r_mask, d_col, 0.0), 0, keepdims=True)
        gram = dot_t(k_b, k_b)
        k_f = k_b.astype(F32)
        q_f = q_b.astype(F32)
        ki_col = lax.rsqrt(jnp.sum(k_f * k_f, 1, keepdims=True) + 1e-06)
        ki_row = lax.rsqrt(jnp.sum(jnp.where(eye, gram, 0.0), 0, keepdims=True) + 1e-06)
        qi_col = lax.rsqrt(jnp.sum(q_f * q_f, 1, keepdims=True) + 1e-06)
        fall = jnp.exp(jnp.minimum(c_col - c_row, 0.0))
        low = jnp.where(lower, gram * (beta_col * ki_col) * ki_row * fall, 0.0)
        reach = dot_t(q_b, k_b) * qi_col * ki_row * fall[:span]
        reach = jnp.where(col_t[:span] <= row_t[:span], reach, 0.0)
        query = q_f * (qi_col * jnp.exp(c_col[:span]))
        work.append((k_b, v_b, beta_row, c_row, c_col, ki_row, ki_col, low, reach, query))

    inverse = [eye_f - jnp.where(levels[0], w[7], 0.0) for w in work]
    for mask in levels[1:]:
        part = [mul(jnp.where(mask, w[7], 0.0), t) for w, t in zip(work, inverse)]
        inverse = [t - mul(t, p) for t, p in zip(inverse, part)]

    states = [None] * heads_in
    for n in range(blocks):
        for i in range(heads_in):
            state = states[i]
            k_b, v_b, beta_row, c_row, c_col, ki_row, ki_col, low, reach, query = work[i * blocks + n]
            t = inverse[i * blocks + n] * beta_row
            written = jnp.concatenate(
                [mul_left(t * (ki_row * jnp.exp(c_row)), k_b), mul_left(t, v_b)], 1
            )
            got = mul(reach, written)
            reduced, local_out = query - got[:, :128], got[:, 128:]
            last = c_col[span - 1 : span, :]
            tail = jnp.exp(last - c_col) * ki_col
            wh, wl = split(written * tail)
            k_t = jnp.transpose(k_b.astype(F32)).astype(BF16)
            made = dot(jnp.concatenate([k_t, k_t], 1), jnp.concatenate([wh, wl], 0))
            trans = jnp.exp(last) * eye_f - made[:, :128]
            inject = made[:, 128:]
            if state is None:
                emit(i, n, reduced, local_out)
                states[i] = jnp.concatenate([trans, inject], 1)
            else:
                read = mul(reduced, state)
                emit(i, n, read[:, :128], read[:, 128:] + local_out)
                states[i] = add_right(mul(trans, state), inject)
    return states


def local_kernel(blocks, q_ref, k_ref, v_ref, s_ref, x_ref, c_ref, b_ref):
    def load(i, n):
        at = pl.ds(n * BLOCK_LEN, BLOCK_LEN)
        k_b = jnp.concatenate([k_ref[0, at, :], k_ref[1, at, :]], 0)
        v_b = jnp.concatenate([v_ref[0, at, :], v_ref[1, at, :]], 0)
        return q_ref[at, :], k_b, v_b, s_ref[0, n : n + 1, :], s_ref[0, blocks + n : blocks + n + 1, :]

    def emit(i, n, carried, base):
        at = pl.ds(n * BLOCK_LEN, BLOCK_LEN)
        c_ref[0, at, :] = carried
        b_ref[0, at, :] = base

    x_ref[0] = head_maps(blocks, 1, load, emit)[0]


def small_rows(betas, log_decay):
    heads, length = log_decay.shape
    blocks = length // BLOCK_LEN
    beta = betas.reshape(2, heads, blocks, BLOCK_LEN).transpose(1, 2, 0, 3)
    beta = beta.reshape(heads, blocks, 2 * BLOCK_LEN)
    decay = log_decay.reshape(heads, blocks, 1, BLOCK_LEN)
    decay = jnp.concatenate([decay, decay], 2).reshape(heads, blocks, 2 * BLOCK_LEN)
    small = jnp.concatenate([decay, beta], 1)
    return small


def local_phase(queries, keys, values, betas, log_decay):
    length = queries.shape[0]
    heads = betas.shape[1]
    blocks = length // BLOCK_LEN
    small = small_rows(betas, log_decay)
    return pl.pallas_call(
        functools.partial(local_kernel, blocks),
        grid=(heads,),
        in_specs=[
            pl.BlockSpec((length, 128), lambda h: (0, h)),
            pl.BlockSpec((2, length, 128), lambda h: (0, 0, h)),
            pl.BlockSpec((2, length, 128), lambda h: (0, 0, h)),
            pl.BlockSpec((1, 2 * blocks, 128), lambda h: (h, 0, 0)),
        ],
        out_specs=[
            pl.BlockSpec((1, 128, 256), lambda h: (h, 0, 0)),
            pl.BlockSpec((1, length, 128), lambda h: (h, 0, 0)),
            pl.BlockSpec((1, length, 128), lambda h: (h, 0, 0)),
        ],
        out_shape=[
            jax.ShapeDtypeStruct((heads, 128, 256), F32),
            jax.ShapeDtypeStruct((heads, length, 128), F32),
            jax.ShapeDtypeStruct((heads, length, 128), F32),
        ],
        name="local_phase",
    )(queries, keys, values, small)


def then(earlier, later):
    return add_right(mul(later[:, :128], earlier), later[:, 128:])


def normed(carried, base, state, gain):
    readout = mul(carried, state) + base
    mean_sq = jnp.mean(readout * readout, 1, keepdims=True)
    return (readout * lax.rsqrt(mean_sq + 1e-05) * gain).astype(BF16)


def whole_kernel(
    inner, outer, q_ref, k_ref, v_ref, s_ref, g_ref, o_ref,
    away, near, own, even_map, sent, got, groups, mine, ready, came, aside, beside, c_buf, b_buf,
    send0, recv0, send1, recv1, send2, recv2, send3, recv3, send4, recv4,
):
    mesh_id = pl.DeviceIdType.MESH
    length = q_ref.shape[0]
    blocks = length // BLOCK_LEN
    me = lax.axis_index("inner")
    group = lax.axis_index("outer")
    core, chip, chips = me % 2, me // 2, inner // 2
    partner = chip * 2 + 1 - core
    groups[...] = jnp.zeros_like(groups)
    barrier = pltpu.get_barrier_semaphore()
    for d in range(1, chips):
        pl.semaphore_signal(
            barrier, inc=1, device_id=(group, (chip + d) % chips * 2 + core), device_id_type=mesh_id
        )
    pl.semaphore_signal(barrier, inc=1, device_id=(group, partner), device_id_type=mesh_id)
    for d in range(1, outer):
        pl.semaphore_signal(barrier, inc=1, device_id=((group + d) % outer, me), device_id_type=mesh_id)
    pl.semaphore_wait(barrier, chips + outer - 1)

    def near_copy(turn):
        return pltpu.make_async_remote_copy(
            src_ref=away.at[turn], dst_ref=near.at[turn],
            send_sem=send0.at[turn], recv_sem=recv0.at[turn],
            device_id=(group, partner), device_id_type=mesh_id,
        )

    def map_copy(d):
        return pltpu.make_async_remote_copy(
            src_ref=sent.at[d], dst_ref=got.at[d],
            send_sem=send1.at[d], recv_sem=recv1.at[d],
            device_id=(group, (chip + d) % chips * 2 + core), device_id_type=mesh_id,
        )

    def chip_map(turn):
        near_copy(turn).wait()
        here, there = own[turn], near[turn]
        even = jnp.where(core == 0, here, there)
        odd = jnp.where(core == 0, there, here)
        even_map[turn] = even
        return then(even, odd)

    def step(turn, carry):
        far = (chip + turn + 1) % chips * 2
        heads = [far + core, far + 1 - core]

        def load(i, n):
            at = pl.ds(n * BLOCK_LEN, BLOCK_LEN)
            lanes = pl.ds(pl.multiple_of(heads[i] * 128, 128), 128)
            k_b = jnp.concatenate([k_ref[0, at, lanes], k_ref[1, at, lanes]], 0)
            v_b = jnp.concatenate([v_ref[0, at, lanes], v_ref[1, at, lanes]], 0)
            rows = s_ref[heads[i]]
            return q_ref[at, lanes], k_b, v_b, rows[n : n + 1], rows[blocks + n : blocks + n + 1]

        def emit(i, n, carried, base):
            at = pl.ds(n * BLOCK_LEN, BLOCK_LEN)
            c_buf[heads[i], at, :] = carried
            b_buf[heads[i], at, :] = base

        states = head_maps(blocks, 2, load, emit)
        away[turn] = states[1]
        near_copy(turn).start()
        own[turn] = states[0]

        @pl.when(turn > 0)
        def _():
            sent[turn] = chip_map(turn - 1)
            map_copy(turn).start()

        return carry

    lax.fori_loop(0, chips, step, 0)
    got[0] = chip_map(chips - 1)
    for d in range(1, chips):
        map_copy(d).wait()

    maps = [got[(chip - i + chips) % chips] for i in range(chips)]

    def tree(parts):
        if len(parts) == 1:
            return parts
        half = len(parts) // 2
        pairs = [then(parts[2 * i], parts[2 * i + 1]) for i in range(half)]
        return pairs

    level = maps
    levels = [maps]
    while len(level) > 1:
        level = tree(level)
        levels.append(level)
    mine[...] = level[0]

    def group_copy(d):
        return pltpu.make_async_remote_copy(
            src_ref=mine, dst_ref=groups.at[d],
            send_sem=send2.at[d], recv_sem=recv2.at[d],
            device_id=((group + d) % outer, me), device_id_type=mesh_id,
        )

    for d in range(1, outer):

        @pl.when(group + d < outer)
        def _():
            group_copy(d).start()

    before = {}
    for i in range(1, chips):
        low = i & -i
        height = low.bit_length() - 1
        part = levels[height][(i - low) >> height]
        before[i] = part if i == low else then(before[i - low], part)
    left = wide(jnp.concatenate([before[i][:, :128] for i in range(1, chips)], 0))
    right = jnp.concatenate([before[i][:, 128:] for i in range(1, chips)], 0)

    for d in range(1, outer):

        @pl.when(group + d < outer)
        def _():
            group_copy(d).wait_send()

        @pl.when(group - d >= 0)
        def _():
            group_copy(d).wait_recv()

    start = jnp.zeros((128, 128), F32)
    for g in range(outer - 1):
        pair = groups[(group - g + outer) % outer]
        moved = mul(pair[:, :128], start) + pair[:, 128:]
        start = jnp.where(g < group, moved, start)

    sh, sl = split(start)
    row = jnp.concatenate([sh, sl], 1)
    both = dot(left, jnp.concatenate([row, row], 0))
    ready[0] = start
    ready[pl.ds(1, chips - 1)] = (both[:, :128] + both[:, 128:] + right).reshape(chips - 1, 128, 128)

    def back_copy(d):
        to = (chip + d) % chips
        return pltpu.make_async_remote_copy(
            src_ref=ready.at[to], dst_ref=came.at[d],
            send_sem=send3.at[d], recv_sem=recv3.at[d],
            device_id=(group, to * 2 + core), device_id_type=mesh_id,
        )

    def side_copy(d):
        return pltpu.make_async_remote_copy(
            src_ref=aside.at[d], dst_ref=beside.at[d],
            send_sem=send4.at[d], recv_sem=recv4.at[d],
            device_id=(group, partner), device_id_type=mesh_id,
        )

    for d in range(1, chips):
        back_copy(d).start()

    def out(head, state):
        lanes = pl.ds(pl.multiple_of(head * 128, 128), 128)
        o_ref[:, lanes] = normed(c_buf[head], b_buf[head], state, g_ref[...])

    for d in range(chips):
        if d:
            back_copy(d).wait()
            enter = came[d]
        else:
            enter = ready[chip]
        pair = even_map[chips - 1 - d]
        after = mul(pair[:, :128], enter) + pair[:, 128:]
        aside[d] = jnp.where(core == 0, after, enter)
        side_copy(d).start()
        far = (chip - d + chips) % chips * 2
        out(far + core, jnp.where(core == 0, enter, after))
        if d:
            side_copy(d - 1).wait()
            out((chip - d + 1 + chips) % chips * 2 + 1 - core, beside[d - 1])
    side_copy(chips - 1).wait()
    out((chip + 1) % chips * 2 + 1 - core, beside[chips - 1])


def whole(inner, outer, queries, keys, values, betas, log_decay, out_gain):
    length, width = queries.shape
    vmem = pl.BlockSpec(memory_space=pltpu.VMEM)
    dma = pltpu.SemaphoreType.DMA
    return pl.pallas_call(
        functools.partial(whole_kernel, inner, outer),
        in_specs=[vmem] * 5,
        out_specs=vmem,
        out_shape=jax.ShapeDtypeStruct((length, width), BF16),
        scratch_shapes=[
            *[pltpu.VMEM((inner // 2, 128, 256), F32)] * 6,
            pltpu.VMEM((outer, 128, 256), F32),
            pltpu.VMEM((128, 256), F32),
            *[pltpu.VMEM((inner // 2, 128, 128), F32)] * 4,
            *[pltpu.VMEM((inner, length, 128), F32)] * 2,
            *[dma((inner // 2,))] * 4,
            *[dma((outer,))] * 2,
            *[dma((inner // 2,))] * 4,
        ],
        compiler_params=pltpu.CompilerParams(collective_id=0, has_side_effects=True),
        name="whole",
    )(queries, keys, values, small_rows(betas, log_decay), out_gain.reshape(1, 128))


HIGHEST = lax.Precision.HIGHEST


def join(earlier, later):
    moved = jnp.einsum("hde,hef->hdf", later[..., :128], earlier, precision=HIGHEST)
    return jnp.concatenate([moved[..., :128], moved[..., 128:] + later[..., 128:]], -1)


def entering(pairs, axis, begin):
    gathered = lax.all_gather(pairs, axis)

    def one(hop, state):
        return join(state, lax.dynamic_index_in_dim(gathered, hop, 0, False))

    return lax.fori_loop(0, lax.axis_index(axis), one, begin)


def exchange_plain(pairs):
    eye = jnp.concatenate([jnp.eye(128, dtype=F32), jnp.zeros((128, 128), F32)], 1)
    begin = jnp.zeros_like(pairs) + eye
    before = entering(pairs, "inner", begin)
    through = join(before, pairs)
    last = lax.axis_index("inner") == lax.axis_size("inner") - 1
    total = lax.psum(jnp.where(last, through, 0.0), "inner")
    start = entering(total, "outer", begin)
    return join(start, before)[..., 128:]


def finish_kernel(c_ref, b_ref, e_ref, g_ref, o_ref):
    readout = mul(c_ref[0], e_ref[0]) + b_ref[0]
    mean_sq = jnp.mean(readout * readout, 1, keepdims=True)
    o_ref[...] = (readout * lax.rsqrt(mean_sq + 1e-05) * g_ref[...]).astype(BF16)


def finish(carried, base, state, out_gain):
    heads, length, _ = carried.shape
    return pl.pallas_call(
        finish_kernel,
        grid=(heads,),
        in_specs=[
            pl.BlockSpec((1, length, 128), lambda h: (h, 0, 0)),
            pl.BlockSpec((1, length, 128), lambda h: (h, 0, 0)),
            pl.BlockSpec((1, 128, 128), lambda h: (h, 0, 0)),
            pl.BlockSpec((1, 128), lambda h: (0, 0)),
        ],
        out_specs=pl.BlockSpec((length, 128), lambda h: (0, h)),
        out_shape=jax.ShapeDtypeStruct((length, heads * 128), BF16),
        name="finish",
    )(carried, base, state, out_gain.reshape(1, 128))


def per_device(inner, outer, queries, keys, values, betas, log_decay, out_gain):
    heads = betas.shape[1]
    if inner == heads:
        return whole(inner, outer, queries, keys, values, betas, log_decay, out_gain)
    pairs, carried, base = local_phase(queries, keys, values, betas, log_decay)
    return finish(carried, base, exchange_plain(pairs), out_gain)


def solution(mesh):
    both = ("outer", "inner")
    placed = (P(both, None), P(None, both, None), P(None, both, None), P(None, None, both), P(None, both), P())
    return jax.shard_map(
        functools.partial(per_device, mesh.shape["inner"], mesh.shape["outer"]),
        mesh=mesh,
        in_specs=placed,
        out_specs=P(both, None),
        check_vma=False,
    )
```
